512 devices in a mesh: kgrp: 16 (over y_hi, x, core), band: 32 (over z, y_lo).
Axes of the slice: x: 4, y: 4 (y_hi: 2, y_lo: 2; y = y_hi * 2 + y_lo), z: 16, core: 2. Of those that a mesh axis runs over, the one named last changes fastest.
Arguments:
- orbitals: bfloat16 [16, 128, 2, 32768], P('kgrp', 'band'), may hold values from -6 to 6
- points: int32 [512], replicated, may hold values from 0 to 32767, as said below
- partner: int32 [16], replicated, may hold values from 0 to 15, each once
- coulomb: bfloat16 [512, 32768], P(None, 'band'), may hold values from -0.01171875 to 0.01171875
Outputs:
- exchange_term: bfloat16 [16, 128, 2, 32768], P('kgrp', 'band')
The draws below stay inside these ranges and needn't reach their ends.
Inputs may be any that keep to these rules, and one draw needn't show every extreme that they name: `points`: 512 distinct grid cells; cells 0 and 32767 are always among them.
All inputs are finite; a program needn't handle non-finite values.
Results may differ from the reference program's by a relative error of at most 0.0057.
Values may be sent and summed in bfloat16 or wider, within the bound.
A program may use at most 64 MiB of HBM per device.

```python
import jax
import jax.numpy as jnp
from jax import lax

NB = 128
GX = 32
GY = 32
GZ = 32
NU = 512
NKG = 16
NG = 32768


def draw_points(key, part):
    first_key, second_key = jax.random.split(jax.random.fold_in(key, 17))
    inner = jax.random.permutation(first_key, NG - 2)[:NU - 2] + 1
    base = jnp.concatenate([jnp.zeros((1,), jnp.int32), inner.astype(jnp.int32), jnp.full((1,), NG - 1, jnp.int32)])
    order = jax.random.permutation(second_key, NU)
    return base[order].astype(jnp.int32)


def level_of(key, extent, cuts, smallest, largest):
    loudness = 1.0
    for dim, parts in cuts:
        steps = jax.random.uniform(jax.random.fold_in(jax.random.fold_in(key, 6), dim), (parts,), jnp.float32, smallest / len(cuts), largest / len(cuts))
        loudness = loudness * jnp.repeat(jnp.exp(steps), extent[dim] // parts).reshape((-1,) + (1,) * (len(extent) - 1 - dim))
    return loudness


def normal_values(stream_key, extent, scale, reach, cuts=(), held_as=jnp.bfloat16):
    array = jax.random.normal(stream_key, extent, jnp.float32) * scale
    if len(cuts) > 0:
        array = level_of(stream_key, extent, cuts, -0.22, 0.18) * array
    return jnp.clip(array, min=-reach, max=reach).astype(held_as)


def setup_inputs(seed: int = 0) -> dict:
    splits = jax.random.split(jax.random.key(seed), 5)
    return {
        "orbitals": normal_values(splits[0], (NKG, NB, 2, NG), 1.0, 6.0, ((0, 16), (1, 32))),
        "points": draw_points(jax.random.fold_in(splits[4], 71), 0),
        "partner": jax.random.permutation(splits[2], NKG).astype(jnp.int32),
        "coulomb": normal_values(splits[3], (NU, NG), (4 * NB * NU) ** -0.5, 0.01171875, ((1, 32),)),
    }


def reference(orbitals, points, partner, coulomb):
    values = jnp.take(orbitals, points, axis=3)
    groups = jnp.arange(NKG, dtype=jnp.int32)
    source = jnp.zeros((NKG,), jnp.int32).at[partner].set(groups)
    coul_f = coulomb.astype(jnp.float32)

    def per_group(group):
        orbital = orbitals[group].astype(jnp.float32)
        own_vals = values[group].astype(jnp.float32)
        src_vals = values[source[group]].astype(jnp.float32)
        turned = jnp.stack([-own_vals[:, 1], own_vals[:, 0]], axis=1)
        own_coef = jnp.stack([own_vals, turned], axis=2)
        density = jnp.einsum('icqm,icr->qmr', own_coef, orbital)
        weighted = (coul_f[None] * density).astype(jnp.bfloat16).astype(jnp.float32)
        src_re = src_vals[:, 0]
        src_im = src_vals[:, 1]
        src_coef = -jnp.stack([jnp.stack([src_re, -src_im], axis=1), jnp.stack([src_im, src_re], axis=1)], axis=1)
        on_grid = jnp.einsum('ipqm,qmr->ipr', src_coef, weighted).astype(jnp.bfloat16).astype(jnp.float32)
        complex_grid = lax.complex(on_grid[:, 0], on_grid[:, 1]).reshape(NB, GX, GY, GZ)
        spectrum = jnp.fft.fftn(complex_grid, axes=(1, 2, 3), norm="ortho").reshape(NB, NG)
        return jnp.stack([jnp.real(spectrum), jnp.imag(spectrum)], axis=1).astype(jnp.bfloat16)

    return lax.map(per_group, groups)
```

```python
import math

import jax
import jax.numpy as jnp
import numpy as np
from jax import lax
from jax.experimental import pallas as pl
from jax.experimental.pallas import tpu as pltpu
from jax.sharding import PartitionSpec as P

MESH = pl.DeviceIdType.MESH
F32 = jnp.float32
BF16 = jnp.bfloat16

NZ = 16
NBAND = 32
NGRP = 16
NU = 512
CELLS = 1024

_DZ = [8]
for _k in range(7, 0, -1):
    _DZ += [_k, -_k]
OFFSETS = [(dz, dy) for dz in _DZ for dy in (0, 1)] + [(0, 1)]


def split_table(table):
    high = jnp.asarray(table, F32).astype(BF16)
    low = (jnp.asarray(table, F32) - high.astype(F32)).astype(BF16)
    return high, low


def plane_tables():
    a = np.arange(8)[:, None, None, None, None]
    u = np.arange(4)[None, :, None, None, None]
    z = np.arange(32)[None, None, :, None, None]
    g = np.arange(4)[None, None, None, :, None]
    kz = np.arange(32)[None, None, None, None, :]
    ky = a + 8 * ((g - a) % 4)
    phase = 2.0 * math.pi / 32.0 * ((ky * u + kz * z) % 32)
    cos_t = (np.cos(phase) / 32.0).reshape(8, 128, 128)
    sin_t = (np.sin(phase) / 32.0).reshape(8, 128, 128)
    return np.concatenate([cos_t, sin_t], axis=2)


def line_table():
    kx = np.arange(32)
    phase = 2.0 * math.pi / 32.0 * (kx[:, None] * kx[None, :] % 32)
    cos_t = np.cos(phase) / math.sqrt(32.0)
    sin_t = np.sin(phase) / math.sqrt(32.0)
    full = np.zeros((2, 4, 32, 32, 2, 4))
    for b in range(4):
        full[0, b, :, :, 0, b] = cos_t
        full[0, b, :, :, 1, b] = sin_t
        full[1, b, :, :, 0, b] = -sin_t
        full[1, b, :, :, 1, b] = cos_t
    return full.reshape(256, 256)


def turn(rows, sign):
    shape = rows.shape
    grouped = rows.reshape(shape[0] // 8, 8, shape[1])
    return (pltpu.roll(grouped, 4, 1) * sign).reshape(shape)


def sign_rows(width):
    row = lax.broadcasted_iota(jnp.int32, (1, 8, width), 1)
    return jnp.where(row < 4, 1.0, -1.0).astype(F32)


def gather_points(x_v, pts_ref, vals):
    pts = pts_ref[...]
    tall = lax.broadcasted_iota(jnp.int32, (512, NU), 0)
    row = 2 * (pts >> 7)
    lane = pts & 127
    data = jnp.concatenate([x_v[b].reshape(512, 128) for b in range(4)], axis=1)
    keep = lax.broadcasted_iota(jnp.int32, (128, NU), 0) == lane
    picked = []
    for c in range(2):
        pick = (tall == row + c).astype(F32).astype(BF16)
        lines = lax.dot_general(data, pick, (((0,), (0,)), ((), ())), preferred_element_type=F32)
        for b in range(4):
            part = jnp.where(keep, lines[b * 128:(b + 1) * 128], 0.0)
            picked.append(jnp.sum(part, axis=0, keepdims=True))
    vals[...] = jnp.concatenate(picked, axis=0).astype(BF16)


def own_matrix(yall, yf, amat):
    for n in range(4):
        yf[...] = yall[:, 0, :, n * 128:(n + 1) * 128].astype(F32).reshape(256, 128)
        parts = [yf[pl.ds(k, 32, stride=8), :] for k in range(8)]
        turned = jnp.transpose(jnp.concatenate(parts, axis=0))
        amat[n * 128:(n + 1) * 128] = turned.astype(BF16)
        crossed = jnp.concatenate([-turned[:, 128:], turned[:, :128]], axis=1)
        amat[NU + n * 128:NU + (n + 1) * 128] = crossed.astype(BF16)


def source_matrix(yall, bmat):
    vals = yall[:, 1].astype(F32).reshape(256, NU)
    bmat[:, 0:NU] = (-vals).astype(BF16)
    bmat[:, NU:2 * NU] = turn(vals, sign_rows(NU)).astype(BF16)


def spread_cells(recv, xf, pmat):
    xf[...] = recv[...].astype(F32).reshape(2048, 128)
    for t in range(8):
        for k in range(8):
            c, b = k // 4, k % 4
            rows = xf[pl.ds(b * 16 + 2 * t + c, 32, stride=64), :]
            pmat[k * 32:(k + 1) * 32, t * 128:(t + 1) * 128] = rows.astype(BF16)


def exchange_cells(amat, bmat, pmat, coul, oscr):
    for n in range(4):
        lanes = slice(n * 256, (n + 1) * 256)
        density = jnp.dot(amat[...], pmat[:, lanes], preferred_element_type=F32)
        fit = coul[:, lanes].astype(F32)
        weighted = jnp.concatenate([fit * density[:NU], fit * density[NU:]], axis=0).astype(BF16)
        oscr[:, lanes] = jnp.dot(bmat[...], weighted, preferred_element_type=F32)


def plane_transform(rows, tab):
    sign = sign_rows(128)
    root = math.sqrt(0.5)
    xs = [rows[:, t * 128:(t + 1) * 128] for t in range(8)]
    even = [xs[t] + xs[t + 4] for t in range(4)]
    odd = [xs[t] - xs[t + 4] for t in range(4)]
    tiles = [None] * 8

    def four(f, first):
        s0, s1, d0 = f[0] + f[2], f[1] + f[3], f[0] - f[2]
        d1 = turn(f[1] - f[3], sign)
        tiles[first] = s0 + s1
        tiles[first + 4] = s0 - s1
        tiles[first + 2] = d0 + d1
        tiles[first + 6] = d0 - d1

    four(even, 0)
    four([
        odd[0],
        (odd[1] + turn(odd[1], sign)) * root,
        turn(odd[2], sign),
        (turn(odd[3], sign) - odd[3]) * root,
    ], 1)
    done = []
    for a in range(8):
        tile = tiles[a].astype(BF16)
        both = jnp.dot(tile, tab[0, a], preferred_element_type=F32)
        both = both + jnp.dot(tile, tab[1, a], preferred_element_type=F32)
        done.append(both[:, :128] + turn(both[:, 128:], sign))
    group = lax.broadcasted_iota(jnp.int32, done[0].shape, 1) >> 5
    outs = []
    for top in range(8):
        half, high = 4 * (top % 2), top // 2
        take = done[half + (0 - high) % 4]
        for g in range(1, 4):
            take = jnp.where(group == g, done[half + (g - high) % 4], take)
        outs.append(pltpu.roll(take, (128 - 32 * high) % 128, 1) if high else take)
    return jnp.concatenate(outs, axis=1)


def line_transform(rz, fx, of, out_ref):
    rows = rz[...].astype(F32).reshape(256, CELLS).astype(BF16)
    full = jnp.dot(fx[0], rows, preferred_element_type=F32)
    full = full + jnp.dot(fx[1], rows, preferred_element_type=F32)
    for t in range(8):
        for p in range(2):
            of[pl.ds(2 * t + p, 128, stride=16), :] = full[p * 128:(p + 1) * 128, t * 128:(t + 1) * 128]
    out_ref[...] = of[...].reshape(4, 32, 16, 128).astype(BF16)


def kernel(x_hbm, pts_ref, partner_ref, coul_hbm, tab_hbm, fx_hbm, out_ref,
           x_v, coul, tab, fx, recv, vals, kbuf, yall, yf, xf, pmat, amat, bmat, oscr, zs, rz, of,
           lsem, asend, arecv, ksend, krecv, psend, precv, msend, mrecv, ysend, yrecv, bsend, brecv):
    me_g = lax.axis_index("kgrp")
    me = lax.axis_index("band")
    z, y = me // 2, me % 2

    def at(dz, dy):
        return ((z + dz + NZ) % NZ) * 2 + (y + dy) % 2

    local = [
        pltpu.make_async_copy(src, dst, lsem.at[n])
        for n, (src, dst) in enumerate(((x_hbm, x_v), (coul_hbm, coul), (tab_hbm, tab), (fx_hbm, fx)))
    ]
    for copy in local:
        copy.start()
    barrier = pltpu.get_barrier_semaphore()

    @pl.loop(1, NBAND)
    def _(k):
        pl.semaphore_signal(barrier, inc=1, device_id={"band": (me + k) % NBAND}, device_id_type=MESH)

    @pl.loop(1, NGRP)
    def _(k):
        pl.semaphore_signal(barrier, inc=1, device_id={"kgrp": (me_g + k) % NGRP}, device_id_type=MESH)

    local[0].wait()
    gather_points(x_v, pts_ref, vals)
    kbuf[me_g] = vals[...]
    yall[me, 0] = vals[...]
    pl.semaphore_wait(barrier, NBAND + NGRP - 2)

    @pl.loop(1, NGRP)
    def _(k):
        pltpu.make_async_remote_copy(
            vals, kbuf.at[me_g], ksend, krecv,
            device_id={"kgrp": (me_g + k) % NGRP}, device_id_type=MESH).start()

    def send_cells(dz, dy):
        to = at(dz, dy)
        pltpu.make_async_remote_copy(
            x_v.at[:, to], recv.at[me], asend, arecv, device_id={"band": to}, device_id_type=MESH).start()

    pltpu.make_async_copy(x_v.at[:, me], recv.at[me], arecv).start()
    for dz, dy in OFFSETS[:7]:
        send_cells(dz, dy)

    pltpu.make_async_copy(kbuf.at[0:NGRP - 1], kbuf.at[0:NGRP - 1], krecv).wait()
    source = jnp.zeros((8, NU), F32)
    for g in range(NGRP):
        hit = jnp.where(partner_ref[g] == me_g, 1.0, 0.0).astype(F32)
        source = source + hit * kbuf[g].astype(F32)
    yall[me, 1] = source.astype(BF16)

    def pass_on(slot, dz, dy, send, arrive):
        pltpu.make_async_remote_copy(
            yall.at[slot], yall.at[slot], send, arrive,
            device_id={"band": at(dz, dy)}, device_id_type=MESH).start()

    def arrived(slot, sem):
        pltpu.make_async_copy(yall.at[slot], yall.at[slot], sem).wait()

    pass_on(me, 1, 0, psend.at[0], precv.at[0])
    pass_on(me, -1, 0, msend.at[0], mrecv.at[0])
    pass_on(me, 0, 1, ysend, yrecv)
    for step in range(1, 9):
        slot = at(-step, 0)
        arrived(slot, precv.at[step - 1])
        if step < 8:
            pass_on(slot, 1, 0, psend.at[step], precv.at[step])
        pass_on(slot, 0, 1, ysend, yrecv)
        if step < 8:
            slot = at(step, 0)
            arrived(slot, mrecv.at[step - 1])
            if step < 7:
                pass_on(slot, -1, 0, msend.at[step], mrecv.at[step])
            pass_on(slot, 0, 1, ysend, yrecv)
        for dz, dy in OFFSETS[4 + 3 * step:7 + 3 * step]:
            send_cells(dz, dy)
    pltpu.make_async_copy(yall.at[0:NZ], yall.at[0:NZ], yrecv).wait()
    own_matrix(yall, yf, amat)
    source_matrix(yall, bmat)

    pltpu.make_async_copy(recv, recv, arecv).wait()
    spread_cells(recv, xf, pmat)
    local[1].wait()
    exchange_cells(amat, bmat, pmat, coul, oscr)
    local[2].wait()

    @pl.loop(0, 4)
    def _(n):
        j = (me // 8 + 2 + n) % 4
        rows = oscr[pl.ds(pl.multiple_of(j * 64, 64), 64), :]
        block = plane_transform(rows, tab).reshape(8, 8, CELLS).astype(BF16)
        zs[pl.ds(j * 8, 8)] = block
        for k in range(8):
            to = j * 8 + k

            @pl.when(to != me)
            def _():
                pltpu.make_async_remote_copy(
                    zs.at[to], rz.at[me], bsend, brecv, device_id={"band": to}, device_id_type=MESH).start()

            @pl.when(to == me)
            def _():
                pltpu.make_async_copy(zs.at[to], rz.at[me], brecv).start()

    local[3].wait()
    pltpu.make_async_copy(rz, rz, brecv).wait()
    line_transform(rz, fx, of, out_ref)

    pltpu.make_async_copy(kbuf.at[0:NGRP - 1], kbuf.at[0:NGRP - 1], ksend).wait()
    pltpu.make_async_copy(recv.at[0:NBAND - 1], recv.at[0:NBAND - 1], asend).wait()
    pltpu.make_async_copy(yall.at[0:NZ], yall.at[0:NZ], ysend).wait()
    for step in range(8):
        arrived(0, psend.at[step])
        if step < 7:
            arrived(0, msend.at[step])
    pltpu.make_async_copy(rz.at[0:NBAND - 1], rz.at[0:NBAND - 1], bsend).wait()


def body(orbitals, points, partner, coulomb):
    tab = jnp.stack(split_table(plane_tables()))
    fx = jnp.stack(split_table(line_table()))
    view = orbitals[0].reshape(4, 2, 32, 8, 128).transpose(0, 2, 3, 1, 4).reshape(4, 32, 16, 128)
    hbm = pl.BlockSpec(memory_space=pl.ANY)
    vmem = pl.BlockSpec(memory_space=pltpu.VMEM)
    dma = pltpu.SemaphoreType.DMA
    out = pl.pallas_call(
        kernel,
        out_shape=jax.ShapeDtypeStruct((4, 32, 16, 128), BF16),
        in_specs=[hbm, vmem, pl.BlockSpec(memory_space=pltpu.SMEM), hbm, hbm, hbm],
        out_specs=vmem,
        scratch_shapes=[
            pltpu.VMEM((4, 32, 16, 128), BF16),
            pltpu.VMEM((NU, CELLS), BF16),
            pltpu.VMEM((2, 8, 128, 256), BF16),
            pltpu.VMEM((2, 256, 256), BF16),
            pltpu.VMEM((NBAND, 4, 16, 128), BF16),
            pltpu.VMEM((8, NU), BF16),
            pltpu.VMEM((NGRP, 8, NU), BF16),
            pltpu.VMEM((NBAND, 2, 8, NU), BF16),
            pltpu.VMEM((256, 128), F32),
            pltpu.VMEM((2048, 128), F32),
            pltpu.VMEM((256, CELLS), BF16),
            pltpu.VMEM((2 * NU, 256), BF16),
            pltpu.VMEM((256, 2 * NU), BF16),
            pltpu.VMEM((256, CELLS), F32),
            pltpu.VMEM((NBAND, 8, CELLS), BF16),
            pltpu.VMEM((NBAND, 8, CELLS), BF16),
            pltpu.VMEM((2048, 128), F32),
            dma((4,)), dma, dma, dma, dma, dma((8,)), dma((8,)), dma((8,)), dma((8,)), dma, dma, dma, dma,
        ],
        compiler_params=pltpu.CompilerParams(
            collective_id=0, has_side_effects=True, vmem_limit_bytes=56 << 20),
    )(view, points.reshape(1, NU), partner, coulomb, tab, fx)
    out = out.reshape(4, 32, 8, 2, 128).transpose(0, 3, 1, 2, 4)
    return out.reshape(1, 4, 2, 32768)


def solution(mesh):
    return jax.shard_map(
        body,
        mesh=mesh,
        in_specs=(P("kgrp", "band", None, None), P(), P(), P(None, "band")),
        out_specs=P("kgrp", "band", None, None),
        check_vma=False,
    )
```

```python
import math

import jax
import jax.numpy as jnp
import numpy as np
from jax import lax
from jax.experimental import pallas as pl
from jax.experimental.pallas import tpu as pltpu
from jax.sharding import PartitionSpec as P

MESH = pl.DeviceIdType.MESH
F32 = jnp.float32
BF16 = jnp.bfloat16

NZ = 16
NBAND = 32
NGRP = 16
NU = 512
CELLS = 1024


def pairs(*steps):
    return [(dz, dy) for dz in steps for dy in (0, 1) if (dz, dy) != (0, 0)]


NEAR = pairs(0, 1, -1, 2, -2, 3, -3, 4, -4)
RELAY = [(4, 0), (-4, 0)]
BATCHES = [pairs(3, -3, 2, -2, 1, -1, 0), pairs(8, 7, -7), pairs(6, -6), pairs(5, -5, 4, -4)]


def split_table(table):
    high = jnp.asarray(table, F32).astype(BF16)
    low = (jnp.asarray(table, F32) - high.astype(F32)).astype(BF16)
    return high, low


def plane_tables():
    a = np.arange(8)[:, None, None, None, None]
    u = np.arange(4)[None, :, None, None, None]
    z = np.arange(32)[None, None, :, None, None]
    g = np.arange(4)[None, None, None, :, None]
    kz = np.arange(32)[None, None, None, None, :]
    ky = a + 8 * ((g - a) % 4)
    phase = 2.0 * math.pi / 32.0 * ((ky * u + kz * z) % 32)
    cos_t = (np.cos(phase) / 32.0).reshape(8, 128, 128)
    sin_t = (np.sin(phase) / 32.0).reshape(8, 128, 128)
    return np.concatenate([cos_t, sin_t], axis=2)


def line_table():
    kx = np.arange(32)
    phase = 2.0 * math.pi / 32.0 * (kx[:, None] * kx[None, :] % 32)
    cos_t = np.cos(phase) / math.sqrt(32.0)
    sin_t = np.sin(phase) / math.sqrt(32.0)
    full = np.zeros((2, 4, 32, 32, 2, 4))
    for b in range(4):
        full[0, b, :, :, 0, b] = cos_t
        full[0, b, :, :, 1, b] = sin_t
        full[1, b, :, :, 0, b] = -sin_t
        full[1, b, :, :, 1, b] = cos_t
    return full.reshape(256, 256)


def turn(rows, sign):
    shape = rows.shape
    grouped = rows.reshape(shape[0] // 8, 8, shape[1])
    return (pltpu.roll(grouped, 4, 1) * sign).reshape(shape)


def sign_rows(width):
    row = lax.broadcasted_iota(jnp.int32, (1, 8, width), 1)
    return jnp.where(row < 4, 1.0, -1.0).astype(F32)


def gather_points(x_v, pts_ref, vals):
    pts = pts_ref[...]
    tall = lax.broadcasted_iota(jnp.int32, (512, NU), 0)
    row = 2 * (pts >> 7)
    lane = pts & 127
    data = jnp.concatenate([x_v[b].reshape(512, 128) for b in range(4)], axis=1)
    keep = lax.broadcasted_iota(jnp.int32, (128, NU), 0) == lane
    picked = []
    for c in range(2):
        pick = (tall == row + c).astype(F32).astype(BF16)
        lines = lax.dot_general(data, pick, (((0,), (0,)), ((), ())), preferred_element_type=F32)
        for b in range(4):
            part = jnp.where(keep, lines[b * 128:(b + 1) * 128], 0.0)
            picked.append(jnp.sum(part, axis=0, keepdims=True))
    vals[...] = jnp.concatenate(picked, axis=0).astype(BF16)


def own_matrix(yall, yf, amat):
    for n in range(4):
        yf[...] = yall[:, :, :, 0, :, n * 128:(n + 1) * 128].astype(F32).reshape(256, 128)
        parts = [yf[pl.ds(k, 32, stride=8), :] for k in range(8)]
        turned = jnp.transpose(jnp.concatenate(parts, axis=0))
        amat[n * 128:(n + 1) * 128] = turned.astype(BF16)
        crossed = jnp.concatenate([-turned[:, 128:], turned[:, :128]], axis=1)
        amat[NU + n * 128:NU + (n + 1) * 128] = crossed.astype(BF16)


def source_matrix(yall, bmat):
    vals = yall[:, :, :, 1].astype(F32).reshape(256, NU)
    bmat[:, 0:NU] = (-vals).astype(BF16)
    bmat[:, NU:2 * NU] = turn(vals, sign_rows(NU)).astype(BF16)


def spread_cells(recv, xf, pmat):
    xf[...] = recv[...].astype(F32).reshape(2048, 128)
    for t in range(8):
        for k in range(8):
            c, b = k // 4, k % 4
            rows = xf[pl.ds(b * 16 + 2 * t + c, 32, stride=64), :]
            pmat[k * 32:(k + 1) * 32, t * 128:(t + 1) * 128] = rows.astype(BF16)


def exchange_cells(amat, bmat, pmat, coul, oscr):
    for n in range(4):
        lanes = slice(n * 256, (n + 1) * 256)
        density = jnp.dot(amat[...], pmat[:, lanes], preferred_element_type=F32)
        fit = coul[:, lanes].astype(F32)
        weighted = jnp.concatenate([fit * density[:NU], fit * density[NU:]], axis=0).astype(BF16)
        oscr[:, lanes] = jnp.dot(bmat[...], weighted, preferred_element_type=F32)


def plane_transform(rows, tab):
    sign = sign_rows(128)
    root = math.sqrt(0.5)
    xs = [rows[:, t * 128:(t + 1) * 128] for t in range(8)]
    even = [xs[t] + xs[t + 4] for t in range(4)]
    odd = [xs[t] - xs[t + 4] for t in range(4)]
    tiles = [None] * 8

    def four(f, first):
        s0, s1, d0 = f[0] + f[2], f[1] + f[3], f[0] - f[2]
        d1 = turn(f[1] - f[3], sign)
        tiles[first] = s0 + s1
        tiles[first + 4] = s0 - s1
        tiles[first + 2] = d0 + d1
        tiles[first + 6] = d0 - d1

    four(even, 0)
    four([
        odd[0],
        (odd[1] + turn(odd[1], sign)) * root,
        turn(odd[2], sign),
        (turn(odd[3], sign) - odd[3]) * root,
    ], 1)
    done = []
    for a in range(8):
        tile = tiles[a].astype(BF16)
        both = jnp.dot(tile, tab[0, a], preferred_element_type=F32)
        both = both + jnp.dot(tile, tab[1, a], preferred_element_type=F32)
        done.append(both[:, :128] + turn(both[:, 128:], sign))
    group = lax.broadcasted_iota(jnp.int32, done[0].shape, 1) >> 5
    outs = []
    for top in range(8):
        half, high = 4 * (top % 2), top // 2
        take = done[half + (0 - high) % 4]
        for g in range(1, 4):
            take = jnp.where(group == g, done[half + (g - high) % 4], take)
        outs.append(pltpu.roll(take, (128 - 32 * high) % 128, 1) if high else take)
    return jnp.concatenate(outs, axis=1)


def line_transform(rz, fx, out_ref, of):
    rows = rz[...].astype(F32).reshape(256, CELLS).astype(BF16)
    full = jnp.dot(fx[0], rows, preferred_element_type=F32)
    full = full + jnp.dot(fx[1], rows, preferred_element_type=F32)
    for t in range(8):
        for p in range(2):
            of[pl.ds(2 * t + p, 128, stride=16), :] = full[p * 128:(p + 1) * 128, t * 128:(t + 1) * 128]
    out_ref[...] = of[...].reshape(4, 32, 16, 128).astype(BF16)


def kernel(x_hbm, pts_ref, partner_ref, coul_hbm, tab_hbm, rz,
           x_v, coul, tab, recv, vals, kbuf, yall, yf, xf, pmat, amat, bmat, oscr, zs,
           lsem, far, asend, arecv, ksend, krecv, gsend, near_recv, group_recv, ysend, yrecv, bsend, brecv):
    me_g = lax.axis_index("kgrp")
    me = lax.axis_index("band")
    z, y = me // 2, me % 2

    def at(dz, dy):
        return ((z + dz + NZ) % NZ) * 2 + (y + dy) % 2

    def band_copy(src, dst, send, arrive, to):
        return pltpu.make_async_remote_copy(
            src, dst, send, arrive, device_id={"band": to}, device_id_type=MESH)

    def await_bytes(ref, sem):
        pltpu.make_async_copy(ref, ref, sem).wait()

    local = [
        pltpu.make_async_copy(src, dst, lsem.at[n])
        for n, (src, dst) in enumerate(((x_hbm, x_v), (coul_hbm, coul), (tab_hbm, tab)))
    ]
    for copy in local:
        copy.start()
    barrier = pltpu.get_barrier_semaphore()

    for dz, dy in NEAR:
        pl.semaphore_signal(barrier, inc=1, device_id={"band": at(dz, dy)}, device_id_type=MESH)

    @pl.loop(1, NGRP)
    def _(k):
        pl.semaphore_signal(barrier, inc=1, device_id={"kgrp": (me_g + k) % NGRP}, device_id_type=MESH)

    local[0].wait()
    gather_points(x_v, pts_ref, vals)
    pl.semaphore_wait(barrier, len(NEAR) + NGRP - 1)
    for dz, dy in RELAY:
        pl.semaphore_signal(far, inc=1, device_id={"band": at(dz, dy)}, device_id_type=MESH)

    @pl.loop(1, NGRP)
    def _(k):
        pltpu.make_async_remote_copy(
            vals, kbuf.at[me_g], ksend, krecv,
            device_id={"kgrp": (me_g + k) % NGRP}, device_id_type=MESH).start()

    def send_cells(offsets):
        for dz, dy in offsets:
            to = at(dz, dy)
            band_copy(x_v.at[:, to], recv.at[me], asend, arecv, to).start()

    send_cells(BATCHES[0])
    pltpu.make_async_copy(x_v.at[:, me], recv.at[me], arecv).start()
    if RELAY:
        pl.semaphore_wait(far, len(RELAY))
    send_cells(BATCHES[1])

    inner, outer = z % 4, z // 4
    kbuf[me_g] = vals[...]
    yall[outer, inner, y, 0] = vals[...]
    await_bytes(kbuf.at[0:NGRP - 1], krecv)
    source = jnp.zeros((8, NU), F32)
    for g in range(NGRP):
        hit = jnp.where(partner_ref[g] == me_g, 1.0, 0.0).astype(F32)
        source = source + hit * kbuf[g].astype(F32)
    yall[outer, inner, y, 1] = source.astype(BF16)

    mine = yall.at[outer, inner, y]
    for dz in (8, 4, -4):
        band_copy(mine, mine, gsend, near_recv, at(dz, 0)).start()
    send_cells(BATCHES[2])
    await_bytes(yall.at[0, 0:3, 0], near_recv)
    group = yall.at[:, inner, y]
    for n, dz in enumerate((2, 1, -1)):
        band_copy(group, group, gsend, group_recv.at[n], at(dz, 0)).start()
    band_copy(group, group, ysend, yrecv, at(0, 1)).start()
    send_cells(BATCHES[3])
    for n, dz in ((1, -1), (2, 1), (0, -2)):
        await_bytes(yall.at[:, 0, 0], group_recv.at[n])
        other = yall.at[:, (inner + dz + 4) % 4, y]
        band_copy(other, other, ysend, yrecv, at(0, 1)).start()
    await_bytes(yall.at[:, :, 0], yrecv)
    own_matrix(yall, yf, amat)
    source_matrix(yall, bmat)

    await_bytes(recv, arecv)
    spread_cells(recv, xf, pmat)
    local[1].wait()
    exchange_cells(amat, bmat, pmat, coul, oscr)
    local[2].wait()

    @pl.loop(0, 4)
    def _(n):
        j = (me // 8 + 2 + n) % 4
        rows = oscr[pl.ds(pl.multiple_of(j * 64, 64), 64), :]
        block = plane_transform(rows, tab).reshape(8, 8, CELLS).astype(BF16)
        zs[pl.ds(j * 8, 8)] = block
        for k in range(8):
            to = j * 8 + k

            @pl.when(to != me)
            def _():
                band_copy(zs.at[to], rz.at[me], bsend, brecv, to).start()

            @pl.when(to == me)
            def _():
                pltpu.make_async_copy(zs.at[to], rz.at[me], brecv).start()

    await_bytes(kbuf.at[0:NGRP - 1], ksend)
    await_bytes(recv.at[0:NBAND - 1], asend)
    await_bytes(yall.at[0, 0:3, 0], gsend)
    await_bytes(yall.at[:, 0:3, 0], gsend)
    await_bytes(yall.at[:, :, 0], ysend)
    await_bytes(rz, brecv)
    await_bytes(rz.at[0:NBAND - 1], bsend)


def body(orbitals, points, partner, coulomb):
    tab = jnp.stack(split_table(plane_tables()))
    fx = jnp.stack(split_table(line_table()))
    view = orbitals[0].reshape(4, 2, 32, 8, 128).transpose(0, 2, 3, 1, 4).reshape(4, 32, 16, 128)
    hbm = pl.BlockSpec(memory_space=pl.ANY)
    vmem = pl.BlockSpec(memory_space=pltpu.VMEM)
    dma = pltpu.SemaphoreType.DMA
    lines = pl.pallas_call(
        kernel,
        out_shape=jax.ShapeDtypeStruct((NBAND, 8, CELLS), BF16),
        in_specs=[hbm, vmem, pl.BlockSpec(memory_space=pltpu.SMEM), hbm, hbm],
        out_specs=hbm,
        scratch_shapes=[
            pltpu.VMEM((4, 32, 16, 128), BF16),
            pltpu.VMEM((NU, CELLS), BF16),
            pltpu.VMEM((2, 8, 128, 256), BF16),
            pltpu.VMEM((NBAND, 4, 16, 128), BF16),
            pltpu.VMEM((8, NU), BF16),
            pltpu.VMEM((NGRP, 8, NU), BF16),
            pltpu.VMEM((4, 4, 2, 2, 8, NU), BF16),
            pltpu.VMEM((256, 128), F32),
            pltpu.VMEM((2048, 128), F32),
            pltpu.VMEM((256, CELLS), BF16),
            pltpu.VMEM((2 * NU, 256), BF16),
            pltpu.VMEM((256, 2 * NU), BF16),
            pltpu.VMEM((256, CELLS), F32),
            pltpu.VMEM((NBAND, 8, CELLS), BF16),
            dma((3,)), pltpu.SemaphoreType.REGULAR, dma, dma, dma, dma, dma, dma, dma((3,)), dma, dma, dma, dma,
        ],
        compiler_params=pltpu.CompilerParams(
            collective_id=0, has_side_effects=True, vmem_limit_bytes=60 << 20),
    )(view, points.reshape(1, NU), partner, coulomb, tab)
    out = pl.pallas_call(
        line_transform,
        out_shape=jax.ShapeDtypeStruct((4, 32, 16, 128), BF16),
        in_specs=[vmem, vmem],
        out_specs=vmem,
        scratch_shapes=[pltpu.VMEM((2048, 128), F32)],
        compiler_params=pltpu.CompilerParams(vmem_limit_bytes=16 << 20),
    )(lines, fx)
    out = out.reshape(4, 32, 8, 2, 128).transpose(0, 3, 1, 2, 4)
    return out.reshape(1, 4, 2, 32768)


def solution(mesh):
    return jax.shard_map(
        body,
        mesh=mesh,
        in_specs=(P("kgrp", "band", None, None), P(), P(), P(None, "band")),
        out_specs=P("kgrp", "band", None, None),
        check_vma=False,
    )
```

```python
import math

import jax
import jax.numpy as jnp
import numpy as np
from jax import lax
from jax.experimental import pallas as pl
from jax.experimental.pallas import tpu as pltpu
from jax.sharding import PartitionSpec as P

MESH = pl.DeviceIdType.MESH
F32 = jnp.float32
BF16 = jnp.bfloat16

NZ = 16
NBAND = 32
NGRP = 16
NU = 512
CELLS = 1024


def pairs(*steps):
    return [(dz, dy) for dz in steps for dy in (0, 1) if (dz, dy) != (0, 0)]


NEAR = pairs(4, -4, 3, -3, 2, -2, 1, -1, 0)
RELAY = [(4, 0), (-4, 0)]
BATCHES = [pairs(3, -3, 2, -2, 1, -1, 0), pairs(8, 7, -7), pairs(6, -6), pairs(5, -5, 4, -4)]


def split_table(table):
    high = jnp.asarray(table, F32).astype(BF16)
    low = (jnp.asarray(table, F32) - high.astype(F32)).astype(BF16)
    return high, low


def plane_tables():
    a = np.arange(8)[:, None, None, None, None]
    u = np.arange(4)[None, :, None, None, None]
    z = np.arange(32)[None, None, :, None, None]
    g = np.arange(4)[None, None, None, :, None]
    kz = np.arange(32)[None, None, None, None, :]
    ky = a + 8 * ((g - a) % 4)
    phase = 2.0 * math.pi / 32.0 * ((ky * u + kz * z) % 32)
    cos_t = (np.cos(phase) / 32.0).reshape(8, 128, 128)
    sin_t = (np.sin(phase) / 32.0).reshape(8, 128, 128)
    return np.concatenate([cos_t, sin_t], axis=2)


def line_table():
    kx = np.arange(32)
    phase = 2.0 * math.pi / 32.0 * (kx[:, None] * kx[None, :] % 32)
    cos_t = np.cos(phase) / math.sqrt(32.0)
    sin_t = np.sin(phase) / math.sqrt(32.0)
    full = np.zeros((2, 4, 32, 32, 2, 4))
    for b in range(4):
        full[0, b, :, :, 0, b] = cos_t
        full[0, b, :, :, 1, b] = sin_t
        full[1, b, :, :, 0, b] = -sin_t
        full[1, b, :, :, 1, b] = cos_t
    return full.reshape(256, 256)


def turn(rows, sign):
    shape = rows.shape
    grouped = rows.reshape(shape[0] // 8, 8, shape[1])
    return (pltpu.roll(grouped, 4, 1) * sign).reshape(shape)


def sign_rows(width):
    row = lax.broadcasted_iota(jnp.int32, (1, 8, width), 1)
    return jnp.where(row < 4, 1.0, -1.0).astype(F32)


def gather_points(x_v, pts_ref, vals):
    pts = pts_ref[...]
    tall = lax.broadcasted_iota(jnp.int32, (512, NU), 0)
    row = 2 * (pts >> 7)
    lane = pts & 127
    data = jnp.concatenate([x_v[b].reshape(512, 128) for b in range(4)], axis=1)
    keep = lax.broadcasted_iota(jnp.int32, (128, NU), 0) == lane
    picked = []
    for c in range(2):
        pick = (tall == row + c).astype(F32).astype(BF16)
        lines = lax.dot_general(data, pick, (((0,), (0,)), ((), ())), preferred_element_type=F32)
        for b in range(4):
            part = jnp.where(keep, lines[b * 128:(b + 1) * 128], 0.0)
            picked.append(jnp.sum(part, axis=0, keepdims=True))
    vals[...] = jnp.concatenate(picked, axis=0).astype(BF16)


def own_matrix(yall, yf, amat):
    for n in range(4):
        yf[...] = yall[:, :, :, 0, :, n * 128:(n + 1) * 128].astype(F32).reshape(256, 128)
        parts = [yf[pl.ds(k, 32, stride=8), :] for k in range(8)]
        turned = jnp.transpose(jnp.concatenate(parts, axis=0))
        amat[n * 128:(n + 1) * 128] = turned.astype(BF16)
        crossed = jnp.concatenate([-turned[:, 128:], turned[:, :128]], axis=1)
        amat[NU + n * 128:NU + (n + 1) * 128] = crossed.astype(BF16)


def source_matrix(yall, bmat):
    vals = yall[:, :, :, 1].astype(F32).reshape(256, NU)
    bmat[:, 0:NU] = (-vals).astype(BF16)
    bmat[:, NU:2 * NU] = turn(vals, sign_rows(NU)).astype(BF16)


def spread_cells(recv, xf, pmat):
    xf[...] = recv[...].astype(F32).reshape(2048, 128)
    for t in range(8):
        for k in range(8):
            c, b = k // 4, k % 4
            rows = xf[pl.ds(b * 16 + 2 * t + c, 32, stride=64), :]
            pmat[k * 32:(k + 1) * 32, t * 128:(t + 1) * 128] = rows.astype(BF16)


def exchange_cells(amat, bmat, pmat, coul, oscr):
    for n in range(4):
        lanes = slice(n * 256, (n + 1) * 256)
        density = jnp.dot(amat[...], pmat[:, lanes], preferred_element_type=F32)
        fit = coul[:, lanes].astype(F32)
        weighted = jnp.concatenate([fit * density[:NU], fit * density[NU:]], axis=0).astype(BF16)
        oscr[:, lanes] = jnp.dot(bmat[...], weighted, preferred_element_type=F32)


def plane_transform(rows, tab):
    sign = sign_rows(128)
    root = math.sqrt(0.5)
    xs = [rows[:, t * 128:(t + 1) * 128] for t in range(8)]
    even = [xs[t] + xs[t + 4] for t in range(4)]
    odd = [xs[t] - xs[t + 4] for t in range(4)]
    tiles = [None] * 8

    def four(f, first):
        s0, s1, d0 = f[0] + f[2], f[1] + f[3], f[0] - f[2]
        d1 = turn(f[1] - f[3], sign)
        tiles[first] = s0 + s1
        tiles[first + 4] = s0 - s1
        tiles[first + 2] = d0 + d1
        tiles[first + 6] = d0 - d1

    four(even, 0)
    four([
        odd[0],
        (odd[1] + turn(odd[1], sign)) * root,
        turn(odd[2], sign),
        (turn(odd[3], sign) - odd[3]) * root,
    ], 1)
    done = []
    for a in range(8):
        tile = tiles[a].astype(BF16)
        both = jnp.dot(tile, tab[0, a], preferred_element_type=F32)
        both = both + jnp.dot(tile, tab[1, a], preferred_element_type=F32)
        done.append(both[:, :128] + turn(both[:, 128:], sign))
    group = lax.broadcasted_iota(jnp.int32, done[0].shape, 1) >> 5
    outs = []
    for top in range(8):
        half, high = 4 * (top % 2), top // 2
        take = done[half + (0 - high) % 4]
        for g in range(1, 4):
            take = jnp.where(group == g, done[half + (g - high) % 4], take)
        outs.append(pltpu.roll(take, (128 - 32 * high) % 128, 1) if high else take)
    return jnp.concatenate(outs, axis=1)


def line_transform(rz, fx, out_ref, of):
    rows = rz[...].astype(F32).reshape(256, CELLS).astype(BF16)
    full = jnp.dot(fx[0], rows, preferred_element_type=F32)
    full = full + jnp.dot(fx[1], rows, preferred_element_type=F32)
    for t in range(8):
        for p in range(2):
            of[pl.ds(2 * t + p, 128, stride=16), :] = full[p * 128:(p + 1) * 128, t * 128:(t + 1) * 128]
    out_ref[...] = of[...].reshape(4, 32, 16, 128).astype(BF16)


def kernel(x_hbm, pts_ref, partner_ref, coul_hbm, tab_hbm, rz,
           x_v, coul, tab, recv, vals, kbuf, yall, yf, xf, pmat, amat, bmat, oscr, zs,
           lsem, far, asend, arecv, ksend, krecv, gsend, near_recv, group_recv, ysend, yrecv, bsend, brecv):
    me_g = lax.axis_index("kgrp")
    me = lax.axis_index("band")
    z, y = me // 2, me % 2

    def at(dz, dy):
        return ((z + dz + NZ) % NZ) * 2 + (y + dy) % 2

    def band_copy(src, dst, send, arrive, to):
        return pltpu.make_async_remote_copy(
            src, dst, send, arrive, device_id={"band": to}, device_id_type=MESH)

    def await_bytes(ref, sem):
        pltpu.make_async_copy(ref, ref, sem).wait()

    local = [
        pltpu.make_async_copy(src, dst, lsem.at[n])
        for n, (src, dst) in enumerate(((x_hbm, x_v), (coul_hbm, coul), (tab_hbm, tab)))
    ]
    for copy in local:
        copy.start()
    barrier = pltpu.get_barrier_semaphore()

    for dz, dy in NEAR:
        pl.semaphore_signal(barrier, inc=1, device_id={"band": at(dz, dy)}, device_id_type=MESH)

    @pl.loop(1, NGRP)
    def _(k):
        pl.semaphore_signal(barrier, inc=1, device_id={"kgrp": (me_g + k) % NGRP}, device_id_type=MESH)

    local[0].wait()
    gather_points(x_v, pts_ref, vals)
    pl.semaphore_wait(barrier, len(NEAR) + NGRP - 1)
    for dz, dy in RELAY:
        pl.semaphore_signal(far, inc=1, device_id={"band": at(dz, dy)}, device_id_type=MESH)

    @pl.loop(1, NGRP)
    def _(k):
        pltpu.make_async_remote_copy(
            vals, kbuf.at[me_g], ksend, krecv,
            device_id={"kgrp": (me_g + k) % NGRP}, device_id_type=MESH).start()

    def send_cells(offsets):
        for dz, dy in offsets:
            to = at(dz, dy)
            band_copy(x_v.at[:, to], recv.at[me], asend, arecv, to).start()

    send_cells(BATCHES[0])
    pltpu.make_async_copy(x_v.at[:, me], recv.at[me], arecv).start()
    if RELAY:
        pl.semaphore_wait(far, len(RELAY))
    send_cells(BATCHES[1])

    inner, outer = z % 4, z // 4
    kbuf[me_g] = vals[...]
    yall[outer, inner, y, 0] = vals[...]
    await_bytes(kbuf.at[0:NGRP - 1], krecv)
    source = jnp.zeros((8, NU), F32)
    for g in range(NGRP):
        hit = jnp.where(partner_ref[g] == me_g, 1.0, 0.0).astype(F32)
        source = source + hit * kbuf[g].astype(F32)
    yall[outer, inner, y, 1] = source.astype(BF16)

    mine = yall.at[outer, inner, y]
    for dz in (8, 4, -4):
        band_copy(mine, mine, gsend, near_recv, at(dz, 0)).start()
    send_cells(BATCHES[2])
    await_bytes(yall.at[0, 0:3, 0], near_recv)
    group = yall.at[:, inner, y]
    for n, dz in enumerate((1, -1)):
        band_copy(group, group, gsend, group_recv.at[n], at(dz, 0)).start()
    for n, dz in enumerate((2, -2)):
        half = yall.at[2 * n:2 * n + 2, inner, y]
        band_copy(half, half, gsend, group_recv.at[2], at(dz, 0)).start()
    band_copy(group, group, ysend, yrecv, at(0, 1)).start()
    send_cells(BATCHES[3])
    for n, dz in enumerate((-1, 1, 2)):
        await_bytes(yall.at[:, 0, 0], group_recv.at[n])
        other = yall.at[:, (inner + dz + 4) % 4, y]
        band_copy(other, other, ysend, yrecv, at(0, 1)).start()
    await_bytes(yall.at[:, :, 0], yrecv)
    own_matrix(yall, yf, amat)
    source_matrix(yall, bmat)

    await_bytes(recv, arecv)
    spread_cells(recv, xf, pmat)
    local[1].wait()
    exchange_cells(amat, bmat, pmat, coul, oscr)
    local[2].wait()

    @pl.loop(0, 4)
    def _(n):
        j = (me // 8 + 2 + n) % 4
        rows = oscr[pl.ds(pl.multiple_of(j * 64, 64), 64), :]
        block = plane_transform(rows, tab).reshape(8, 8, CELLS).astype(BF16)
        zs[pl.ds(j * 8, 8)] = block
        for k in range(8):
            to = j * 8 + k

            @pl.when(to != me)
            def _():
                band_copy(zs.at[to], rz.at[me], bsend, brecv, to).start()

            @pl.when(to == me)
            def _():
                pltpu.make_async_copy(zs.at[to], rz.at[me], brecv).start()

    await_bytes(kbuf.at[0:NGRP - 1], ksend)
    await_bytes(recv.at[0:NBAND - 1], asend)
    await_bytes(yall.at[0, 0:3, 0], gsend)
    await_bytes(yall.at[:, 0:3, 0], gsend)
    await_bytes(yall.at[:, :, 0], ysend)
    await_bytes(rz, brecv)
    await_bytes(rz.at[0:NBAND - 1], bsend)


def body(orbitals, points, partner, coulomb):
    tab = jnp.stack(split_table(plane_tables()))
    fx = jnp.stack(split_table(line_table()))
    view = orbitals[0].reshape(4, 2, 32, 8, 128).transpose(0, 2, 3, 1, 4).reshape(4, 32, 16, 128)
    hbm = pl.BlockSpec(memory_space=pl.ANY)
    vmem = pl.BlockSpec(memory_space=pltpu.VMEM)
    dma = pltpu.SemaphoreType.DMA
    lines = pl.pallas_call(
        kernel,
        out_shape=jax.ShapeDtypeStruct((NBAND, 8, CELLS), BF16),
        in_specs=[hbm, vmem, pl.BlockSpec(memory_space=pltpu.SMEM), hbm, hbm],
        out_specs=hbm,
        scratch_shapes=[
            pltpu.VMEM((4, 32, 16, 128), BF16),
            pltpu.VMEM((NU, CELLS), BF16),
            pltpu.VMEM((2, 8, 128, 256), BF16),
            pltpu.VMEM((NBAND, 4, 16, 128), BF16),
            pltpu.VMEM((8, NU), BF16),
            pltpu.VMEM((NGRP, 8, NU), BF16),
            pltpu.VMEM((4, 4, 2, 2, 8, NU), BF16),
            pltpu.VMEM((256, 128), F32),
            pltpu.VMEM((2048, 128), F32),
            pltpu.VMEM((256, CELLS), BF16),
            pltpu.VMEM((2 * NU, 256), BF16),
            pltpu.VMEM((256, 2 * NU), BF16),
            pltpu.VMEM((256, CELLS), F32),
            pltpu.VMEM((NBAND, 8, CELLS), BF16),
            dma((3,)), pltpu.SemaphoreType.REGULAR, dma, dma, dma, dma, dma, dma, dma((3,)), dma, dma, dma, dma,
        ],
        compiler_params=pltpu.CompilerParams(
            collective_id=0, has_side_effects=True, vmem_limit_bytes=60 << 20),
    )(view, points.reshape(1, NU), partner, coulomb, tab)
    out = pl.pallas_call(
        line_transform,
        out_shape=jax.ShapeDtypeStruct((4, 32, 16, 128), BF16),
        in_specs=[vmem, vmem],
        out_specs=vmem,
        scratch_shapes=[pltpu.VMEM((2048, 128), F32)],
        compiler_params=pltpu.CompilerParams(vmem_limit_bytes=16 << 20),
    )(lines, fx)
    out = out.reshape(4, 32, 8, 2, 128).transpose(0, 3, 1, 2, 4)
    return out.reshape(1, 4, 2, 32768)


def solution(mesh):
    return jax.shard_map(
        body,
        mesh=mesh,
        in_specs=(P("kgrp", "band", None, None), P(), P(), P(None, "band")),
        out_specs=P("kgrp", "band", None, None),
        check_vma=False,
    )
```

```python
import math

import jax
import jax.numpy as jnp
import numpy as np
from jax import lax
from jax.experimental import pallas as pl
from jax.experimental.pallas import tpu as pltpu
from jax.sharding import PartitionSpec as P

MESH = pl.DeviceIdType.MESH
F32 = jnp.float32
BF16 = jnp.bfloat16

NZ = 16
NBAND = 32
NGRP = 16
NU = 512
CELLS = 1024


def pairs(*steps):
    return [(dz, dy) for dz in steps for dy in (0, 1) if (dz, dy) != (0, 0)]


NEAR = pairs(4, -4, 3, -3, 2, -2, 1, -1, 0)
RELAY = [(4, 0), (-4, 0)]
BATCHES = [pairs(3, -3, 2, -2, 1, -1, 0), pairs(8, 7, -7), pairs(6, -6), pairs(5, -5, 4, -4)]


def split_table(table):
    high = jnp.asarray(table, F32).astype(BF16)
    low = (jnp.asarray(table, F32) - high.astype(F32)).astype(BF16)
    return high, low


def plane_tables():
    a = np.arange(8)[:, None, None, None, None]
    u = np.arange(4)[None, :, None, None, None]
    z = np.arange(32)[None, None, :, None, None]
    g = np.arange(4)[None, None, None, :, None]
    kz = np.arange(32)[None, None, None, None, :]
    ky = a + 8 * ((g - a) % 4)
    phase = 2.0 * math.pi / 32.0 * ((ky * u + kz * z) % 32)
    cos_t = (np.cos(phase) / 32.0).reshape(8, 128, 128)
    sin_t = (np.sin(phase) / 32.0).reshape(8, 128, 128)
    return np.concatenate([cos_t, sin_t], axis=2)


def line_table():
    kx = np.arange(32)
    phase = 2.0 * math.pi / 32.0 * (kx[:, None] * kx[None, :] % 32)
    cos_t = np.cos(phase) / math.sqrt(32.0)
    sin_t = np.sin(phase) / math.sqrt(32.0)
    full = np.zeros((2, 4, 32, 32, 2, 4))
    for b in range(4):
        full[0, b, :, :, 0, b] = cos_t
        full[0, b, :, :, 1, b] = sin_t
        full[1, b, :, :, 0, b] = -sin_t
        full[1, b, :, :, 1, b] = cos_t
    return full.reshape(256, 256)


def turn(rows, sign):
    shape = rows.shape
    grouped = rows.reshape(shape[0] // 8, 8, shape[1])
    return (pltpu.roll(grouped, 4, 1) * sign).reshape(shape)


def sign_rows(width):
    row = lax.broadcasted_iota(jnp.int32, (1, 8, width), 1)
    return jnp.where(row < 4, 1.0, -1.0).astype(F32)


def gather_points(x_v, pts_ref, vals):
    pts = pts_ref[...]
    tall = lax.broadcasted_iota(jnp.int32, (512, NU), 0)
    row = 2 * (pts >> 7)
    lane = pts & 127
    data = jnp.concatenate([x_v[b].reshape(512, 128) for b in range(4)], axis=1)
    keep = lax.broadcasted_iota(jnp.int32, (128, NU), 0) == lane
    picked = []
    for c in range(2):
        pick = (tall == row + c).astype(F32).astype(BF16)
        lines = lax.dot_general(data, pick, (((0,), (0,)), ((), ())), preferred_element_type=F32)
        for b in range(4):
            part = jnp.where(keep, lines[b * 128:(b + 1) * 128], 0.0)
            picked.append(jnp.sum(part, axis=0, keepdims=True))
    vals[...] = jnp.concatenate(picked, axis=0).astype(BF16)


def own_matrix(yall, yf, amat):
    for n in range(4):
        yf[...] = yall[:, :, :, 0, :, n * 128:(n + 1) * 128].astype(F32).reshape(256, 128)
        parts = [yf[pl.ds(k, 32, stride=8), :] for k in range(8)]
        turned = jnp.transpose(jnp.concatenate(parts, axis=0))
        amat[n * 128:(n + 1) * 128] = turned.astype(BF16)
        crossed = jnp.concatenate([-turned[:, 128:], turned[:, :128]], axis=1)
        amat[NU + n * 128:NU + (n + 1) * 128] = crossed.astype(BF16)


def source_matrix(yall, bmat):
    vals = yall[:, :, :, 1].astype(F32).reshape(256, NU)
    bmat[:, 0:NU] = (-vals).astype(BF16)
    bmat[:, NU:2 * NU] = turn(vals, sign_rows(NU)).astype(BF16)


def spread_cells(recv, xf, pmat):
    xf[...] = recv[...].astype(F32).reshape(2048, 128)
    for t in range(8):
        for k in range(8):
            c, b = k // 4, k % 4
            rows = xf[pl.ds(b * 16 + 2 * t + c, 32, stride=64), :]
            pmat[k * 32:(k + 1) * 32, t * 128:(t + 1) * 128] = rows.astype(BF16)


def exchange_cells(amat, bmat, pmat, coul, oscr):
    for n in range(4):
        lanes = slice(n * 256, (n + 1) * 256)
        density = jnp.dot(amat[...], pmat[:, lanes], preferred_element_type=F32)
        fit = coul[:, lanes].astype(F32)
        weighted = jnp.concatenate([fit * density[:NU], fit * density[NU:]], axis=0).astype(BF16)
        oscr[:, lanes] = jnp.dot(bmat[...], weighted, preferred_element_type=F32)


def plane_transform(rows, tab):
    sign = sign_rows(128)
    root = math.sqrt(0.5)
    xs = [rows[:, t * 128:(t + 1) * 128] for t in range(8)]
    even = [xs[t] + xs[t + 4] for t in range(4)]
    odd = [xs[t] - xs[t + 4] for t in range(4)]
    tiles = [None] * 8

    def four(f, first):
        s0, s1, d0 = f[0] + f[2], f[1] + f[3], f[0] - f[2]
        d1 = turn(f[1] - f[3], sign)
        tiles[first] = s0 + s1
        tiles[first + 4] = s0 - s1
        tiles[first + 2] = d0 + d1
        tiles[first + 6] = d0 - d1

    four(even, 0)
    four([
        odd[0],
        (odd[1] + turn(odd[1], sign)) * root,
        turn(odd[2], sign),
        (turn(odd[3], sign) - odd[3]) * root,
    ], 1)
    done = []
    for a in range(8):
        tile = tiles[a].astype(BF16)
        both = jnp.dot(tile, tab[0, a], preferred_element_type=F32)
        both = both + jnp.dot(tile, tab[1, a], preferred_element_type=F32)
        done.append(both[:, :128] + turn(both[:, 128:], sign))
    group = lax.broadcasted_iota(jnp.int32, done[0].shape, 1) >> 5
    outs = []
    for top in range(8):
        half, high = 4 * (top % 2), top // 2
        take = done[half + (0 - high) % 4]
        for g in range(1, 4):
            take = jnp.where(group == g, done[half + (g - high) % 4], take)
        outs.append(pltpu.roll(take, (128 - 32 * high) % 128, 1) if high else take)
    return jnp.concatenate(outs, axis=1)


def line_transform(rz, fx, out_ref, of):
    rows = rz[...].astype(F32).reshape(256, CELLS).astype(BF16)
    full = jnp.dot(fx[0], rows, preferred_element_type=F32)
    full = full + jnp.dot(fx[1], rows, preferred_element_type=F32)
    for t in range(8):
        for p in range(2):
            of[pl.ds(2 * t + p, 128, stride=16), :] = full[p * 128:(p + 1) * 128, t * 128:(t + 1) * 128]
    out_ref[...] = of[...].reshape(4, 32, 16, 128).astype(BF16)


def kernel(x_hbm, pts_ref, partner_ref, coul_hbm, tab_hbm, rz,
           x_v, coul, tab, recv, vals, kbuf, yall, yf, xf, pmat, amat, bmat, oscr, zs,
           lsem, far, asend, arecv, ksend, krecv, gsend, near_recv, group_recv, ysend, yrecv, bsend, brecv):
    me_g = lax.axis_index("kgrp")
    me = lax.axis_index("band")
    z, y = me // 2, me % 2

    def at(dz, dy):
        return ((z + dz + NZ) % NZ) * 2 + (y + dy) % 2

    def band_copy(src, dst, send, arrive, to):
        return pltpu.make_async_remote_copy(
            src, dst, send, arrive, device_id={"band": to}, device_id_type=MESH)

    def await_bytes(ref, sem):
        pltpu.make_async_copy(ref, ref, sem).wait()

    local = [
        pltpu.make_async_copy(src, dst, lsem.at[n])
        for n, (src, dst) in enumerate(((x_hbm, x_v), (coul_hbm, coul), (tab_hbm, tab)))
    ]
    barrier = pltpu.get_barrier_semaphore()

    for dz, dy in NEAR:
        pl.semaphore_signal(barrier, inc=1, device_id={"band": at(dz, dy)}, device_id_type=MESH)

    @pl.loop(1, NGRP)
    def _(k):
        pl.semaphore_signal(barrier, inc=1, device_id={"kgrp": (me_g + k) % NGRP}, device_id_type=MESH)

    for copy in local:
        copy.start()
    local[0].wait()
    pltpu.make_async_copy(x_v.at[:, me], recv.at[me], arecv).start()
    gather_points(x_v, pts_ref, vals)
    inner, outer = z % 4, z // 4
    kbuf[me_g] = vals[...]
    yall[outer, inner, y, 0] = vals[...]
    pl.semaphore_wait(barrier, len(NEAR) + NGRP - 1)
    for dz, dy in RELAY:
        pl.semaphore_signal(far, inc=1, device_id={"band": at(dz, dy)}, device_id_type=MESH)

    @pl.loop(1, NGRP)
    def _(k):
        pltpu.make_async_remote_copy(
            vals, kbuf.at[me_g], ksend, krecv,
            device_id={"kgrp": (me_g + k) % NGRP}, device_id_type=MESH).start()

    def send_cells(offsets):
        for dz, dy in offsets:
            to = at(dz, dy)
            band_copy(x_v.at[:, to], recv.at[me], asend, arecv, to).start()

    send_cells(BATCHES[0])
    if RELAY:
        pl.semaphore_wait(far, len(RELAY))
    send_cells(BATCHES[1])

    await_bytes(kbuf.at[0:NGRP - 1], krecv)
    source = jnp.zeros((8, NU), F32)
    for g in range(NGRP):
        hit = jnp.where(partner_ref[g] == me_g, 1.0, 0.0).astype(F32)
        source = source + hit * kbuf[g].astype(F32)
    yall[outer, inner, y, 1] = source.astype(BF16)

    mine = yall.at[outer, inner, y]
    for dz in (8, 4, -4):
        band_copy(mine, mine, gsend, near_recv, at(dz, 0)).start()
    send_cells(BATCHES[2])
    await_bytes(yall.at[0, 0:3, 0], near_recv)
    group = yall.at[:, inner, y]
    for n, dz in enumerate((1, -1)):
        band_copy(group, group, gsend, group_recv.at[n], at(dz, 0)).start()
    for n, dz in enumerate((2, -2)):
        half = yall.at[2 * n:2 * n + 2, inner, y]
        band_copy(half, half, gsend, group_recv.at[2], at(dz, 0)).start()
    band_copy(group, group, ysend, yrecv, at(0, 1)).start()
    send_cells(BATCHES[3])
    for n, dz in enumerate((-1, 1, 2)):
        await_bytes(yall.at[:, 0, 0], group_recv.at[n])
        other = yall.at[:, (inner + dz + 4) % 4, y]
        band_copy(other, other, ysend, yrecv, at(0, 1)).start()
    await_bytes(yall.at[:, :, 0], yrecv)
    own_matrix(yall, yf, amat)
    source_matrix(yall, bmat)

    await_bytes(recv, arecv)
    spread_cells(recv, xf, pmat)
    local[1].wait()
    exchange_cells(amat, bmat, pmat, coul, oscr)
    local[2].wait()

    @pl.loop(0, 4)
    def _(n):
        j = (me // 8 + 2 + n) % 4
        rows = oscr[pl.ds(pl.multiple_of(j * 64, 64), 64), :]
        block = plane_transform(rows, tab).reshape(8, 8, CELLS).astype(BF16)
        zs[pl.ds(j * 8, 8)] = block
        for k in range(8):
            to = j * 8 + k

            @pl.when(to != me)
            def _():
                band_copy(zs.at[to], rz.at[me], bsend, brecv, to).start()

            @pl.when(to == me)
            def _():
                pltpu.make_async_copy(zs.at[to], rz.at[me], brecv).start()

    await_bytes(kbuf.at[0:NGRP - 1], ksend)
    await_bytes(recv.at[0:NBAND - 1], asend)
    await_bytes(yall.at[0, 0:3, 0], gsend)
    await_bytes(yall.at[:, 0:3, 0], gsend)
    await_bytes(yall.at[:, :, 0], ysend)
    await_bytes(rz, brecv)
    await_bytes(rz.at[0:NBAND - 1], bsend)


def body(orbitals, points, partner, coulomb):
    tab = jnp.stack(split_table(plane_tables()))
    fx = jnp.stack(split_table(line_table()))
    view = orbitals[0].reshape(4, 2, 32, 8, 128).transpose(0, 2, 3, 1, 4).reshape(4, 32, 16, 128)
    hbm = pl.BlockSpec(memory_space=pl.ANY)
    vmem = pl.BlockSpec(memory_space=pltpu.VMEM)
    dma = pltpu.SemaphoreType.DMA
    lines = pl.pallas_call(
        kernel,
        out_shape=jax.ShapeDtypeStruct((NBAND, 8, CELLS), BF16),
        in_specs=[hbm, vmem, pl.BlockSpec(memory_space=pltpu.SMEM), hbm, hbm],
        out_specs=hbm,
        scratch_shapes=[
            pltpu.VMEM((4, 32, 16, 128), BF16),
            pltpu.VMEM((NU, CELLS), BF16),
            pltpu.VMEM((2, 8, 128, 256), BF16),
            pltpu.VMEM((NBAND, 4, 16, 128), BF16),
            pltpu.VMEM((8, NU), BF16),
            pltpu.VMEM((NGRP, 8, NU), BF16),
            pltpu.VMEM((4, 4, 2, 2, 8, NU), BF16),
            pltpu.VMEM((256, 128), F32),
            pltpu.VMEM((2048, 128), F32),
            pltpu.VMEM((256, CELLS), BF16),
            pltpu.VMEM((2 * NU, 256), BF16),
            pltpu.VMEM((256, 2 * NU), BF16),
            pltpu.VMEM((256, CELLS), F32),
            pltpu.VMEM((NBAND, 8, CELLS), BF16),
            dma((3,)), pltpu.SemaphoreType.REGULAR, dma, dma, dma, dma, dma, dma, dma((3,)), dma, dma, dma, dma,
        ],
        compiler_params=pltpu.CompilerParams(
            collective_id=0, has_side_effects=True, vmem_limit_bytes=60 << 20),
    )(view, points.reshape(1, NU), partner, coulomb, tab)
    out = pl.pallas_call(
        line_transform,
        out_shape=jax.ShapeDtypeStruct((4, 32, 16, 128), BF16),
        in_specs=[vmem, vmem],
        out_specs=vmem,
        scratch_shapes=[pltpu.VMEM((2048, 128), F32)],
        compiler_params=pltpu.CompilerParams(vmem_limit_bytes=16 << 20),
    )(lines, fx)
    out = out.reshape(4, 32, 8, 2, 128).transpose(0, 3, 1, 2, 4)
    return out.reshape(1, 4, 2, 32768)


def solution(mesh):
    return jax.shard_map(
        body,
        mesh=mesh,
        in_specs=(P("kgrp", "band", None, None), P(), P(), P(None, "band")),
        out_specs=P("kgrp", "band", None, None),
        check_vma=False,
    )
```
